1024 devices in a mesh: gx: 32 (over z, core), gy: 4 (over x), gz: 8 (over y).
Axes of the slice: x: 4, y: 8, z: 16, core: 2. Of those that a mesh axis runs over, the one named last changes fastest.
Arguments:
- loads: float32 [128, 655360], P(None, ('gx', 'gy', 'gz')), may hold values from -6 to 6
- stiffness: bfloat16 [655360, 640], P(('gx', 'gy', 'gz')), may hold values from -1 to 3
- stiff_inverse: bfloat16 [655360, 640], P(('gx', 'gy', 'gz')), may hold values from -1 to 1
- face_rows: int32 [1024, 6, 96], P(('gx', 'gy', 'gz')), may hold values from 0 to 639, as said below
- coarse_basis: bfloat16 [196608, 640], P(('gx', 'gy', 'gz')), may hold values from -0.25 to 0.25
- coarse_map: int32 [1024, 192], P(('gx', 'gy', 'gz')), may hold values from 0 to 1535, as said below
- group_rows: bfloat16 [196608, 1536], P(('gx', 'gy', 'gz')), may hold values from -1 to 1, as said below
- root_coupling: bfloat16 [196608, 512], P(('gx', 'gy', 'gz')), may hold values from -1 to 1
- root_inverse: bfloat16 [512, 512], replicated, may hold values from -0.013671875 to 0.013671875
Outputs:
- solution: float32 [128, 655360], P(None, ('gx', 'gy', 'gz'))
- residual: float32 [128, 655360], P(None, ('gx', 'gy', 'gz'))
The draws below stay inside these ranges and needn't reach their ends.
Inputs may be any that keep to these rules, and one draw needn't show every extreme that they name: `face_rows`: for every subdomain the 6 x 96 entries are distinct; entry i of a face and entry i of the opposite face of the neighbour across it name the same shared dof. `coarse_map`: the 192 entries of a subdomain are distinct. `group_rows`: row i of a subdomain's block is row coarse_map[s, i] of one symmetric matrix of its group; children naming the same group dof hold the same row.
All inputs are finite; a program needn't handle non-finite values.
Results may differ from the reference program's by a relative error of at most 0.014.
Values may be sent and summed in bfloat16 or wider, within the bound.
No kernel may reach another device: no remote copies, remote signals or barrier semaphores. Data moves between devices by JAX's collectives and lax.ppermute only.
A program may use at most 32 MiB of HBM per device.

```python
import jax
import jax.numpy as jnp
from jax import lax

INTERFACE = 640
FACE_DOFS = 96
COARSE = 192
GROUP_DOFS = 1536
ROOT_DOFS = 512
COLUMNS = 128
SUBDOMAINS = 1024
CHILDREN = 32
GROUPS = 32
N_GX = 32
N_GY = 4
N_GZ = 8


def stiff_block(block_key):
    first_key, second_key = jax.random.split(block_key)
    diagonal = jax.random.uniform(first_key, (INTERFACE,), jnp.float32, 1.0, 3.0)
    raw = jax.random.normal(second_key, (INTERFACE, INTERFACE), jnp.float32) * (0.3 * (2.0 / INTERFACE) ** 0.5)
    identity = jnp.eye(INTERFACE, dtype=jnp.float32)
    offdiag = 0.5 * (raw + raw.T) * (1.0 - identity)
    stiff = offdiag + identity * diagonal[:, None]
    inverse = identity / diagonal[:, None] - offdiag / (diagonal[:, None] * diagonal[None, :])
    return (stiff.astype(jnp.bfloat16), inverse.astype(jnp.bfloat16))


def stiff_pair(key):
    block_keys = jax.random.split(jax.random.fold_in(key, 7), SUBDOMAINS)
    stiff, inverse = lax.map(stiff_block, block_keys)
    return (stiff.reshape(SUBDOMAINS * INTERFACE, INTERFACE), inverse.reshape(SUBDOMAINS * INTERFACE, INTERFACE))


def draw_stiffness(key, part):
    return stiff_pair(key)[0]


def draw_stiff_inverse(key, part):
    return stiff_pair(key)[1]


def draw_face_rows(key, part):
    block_keys = jax.random.split(jax.random.fold_in(key, 21), SUBDOMAINS)
    chosen = jax.vmap(lambda block: jax.random.permutation(block, INTERFACE)[:6 * FACE_DOFS])(block_keys)
    return chosen.reshape(SUBDOMAINS, 6, FACE_DOFS).astype(jnp.int32)


def coarse_maps(key):
    block_keys = jax.random.split(jax.random.fold_in(key, 31), SUBDOMAINS)
    chosen = jax.vmap(lambda block: jax.random.permutation(block, GROUP_DOFS)[:COARSE])(block_keys)
    return chosen.astype(jnp.int32)


def draw_coarse_map(key, part):
    return coarse_maps(key)


def draw_group_rows(key, part):
    mapping = coarse_maps(key)
    first_key, second_key = jax.random.split(jax.random.fold_in(key, 41))
    diagonal = jax.random.uniform(first_key, (GROUPS, GROUP_DOFS), jnp.float32, 0.2, 0.4)
    raw = jax.random.normal(second_key, (GROUPS, GROUP_DOFS, GROUP_DOFS), jnp.float32) * (0.3 * (2.0 / GROUP_DOFS) ** 0.5)
    identity = jnp.eye(GROUP_DOFS, dtype=jnp.float32)
    matrices = 0.5 * (raw + jnp.swapaxes(raw, 1, 2)) * (1.0 - identity) + identity * diagonal[:, :, None]
    group_index = (jnp.arange(SUBDOMAINS) % GROUPS).astype(jnp.int32)
    picked = lax.map(lambda operands: jnp.take(matrices[operands[0]], operands[1], axis=0), (group_index, mapping))
    return picked.reshape(SUBDOMAINS * COARSE, GROUP_DOFS).astype(jnp.bfloat16)


def spiked(drawn, key, source, target, parts, factor):
    owner, partner = [(jnp.arange(drawn.shape[dim]) // (drawn.shape[dim] // parts)).reshape([-1 if axis == dim else 1 for axis in range(drawn.ndim)]) for dim in (source, target)]
    chosen = jax.random.permutation(key, parts)[partner]
    strong = (owner == chosen) | (owner == (partner + parts // 2) % parts)
    return jnp.where(strong, factor * drawn, drawn)


def shard_levels(rng, dims, cuts, least, largest):
    loudness, own = 1.0, jax.random.fold_in(rng, 6)
    for axis_at, shards_of in cuts:
        steps = jnp.exp(jax.random.uniform(jax.random.fold_in(own, axis_at), (shards_of,), jnp.float32, least / len(cuts), largest / len(cuts)))
        loudness = loudness * jnp.repeat(steps, dims[axis_at] // shards_of).reshape([-1 if axis == axis_at else 1 for axis in range(len(dims))])
    return loudness


def bell_draw(key, shape, spread, most, shards=(), kind=jnp.bfloat16):
    entries = spread * jax.random.normal(key, shape, jnp.float32)
    if shards:
        entries = entries * shard_levels(key, shape, shards, -0.22, 0.18)
    return jnp.clip(entries, -most, most).astype(kind)


def heavy_noise(key, shape, deviation, most, cuts, heavy, held_as=jnp.bfloat16):
    entries = deviation * jax.random.normal(key, shape, jnp.float32)
    if cuts:
        entries = entries * shard_levels(key, shape, cuts, -0.22, 0.18)
    return jnp.clip(spiked(entries, jax.random.fold_in(key, 3), *heavy), -most, most).astype(held_as)


def setup_inputs(seed: int = 0) -> dict:
    arg_keys = jax.random.split(jax.random.key(seed), 10)
    loads = bell_draw(arg_keys[0], (COLUMNS, SUBDOMAINS * INTERFACE), 1.0, 6.0, ((1, 1024),), jnp.float32)
    stiffness = draw_stiffness(jax.random.fold_in(arg_keys[9], 71), 0)
    stiff_inverse = draw_stiff_inverse(jax.random.fold_in(arg_keys[9], 71), 0)
    face_rows = draw_face_rows(jax.random.fold_in(arg_keys[9], 71), 0)
    coarse_basis = bell_draw(arg_keys[4], (SUBDOMAINS * COARSE, INTERFACE), INTERFACE ** -0.5, 0.25, ((0, 1024),))
    coarse_map = draw_coarse_map(jax.random.fold_in(arg_keys[9], 71), 0)
    group_rows = draw_group_rows(jax.random.fold_in(arg_keys[9], 71), 0)
    root_coupling = heavy_noise(arg_keys[7], (SUBDOMAINS * COARSE, ROOT_DOFS), ROOT_DOFS ** -0.5, 1.0, ((0, 1024),), (0, 1, 512, 6.0))
    root_inverse = bell_draw(arg_keys[8], (ROOT_DOFS, ROOT_DOFS), (SUBDOMAINS * COARSE) ** -0.5, 0.013671875)
    return {"loads": loads, "stiffness": stiffness, "stiff_inverse": stiff_inverse, "face_rows": face_rows, "coarse_basis": coarse_basis, "coarse_map": coarse_map, "group_rows": group_rows, "root_coupling": root_coupling, "root_inverse": root_inverse}


def split_subs(field):
    return field.reshape(COLUMNS, SUBDOMAINS, INTERFACE).transpose(1, 0, 2)


def join_subs(field):
    return field.transpose(1, 0, 2).reshape(COLUMNS, SUBDOMAINS * INTERFACE)


def from_lower(values, axis):
    size = values.shape[axis]
    edge = jnp.zeros_like(lax.slice_in_dim(values, 0, 1, axis=axis))
    return jnp.concatenate([edge, lax.slice_in_dim(values, 0, size - 1, axis=axis)], axis)


def from_upper(values, axis):
    size = values.shape[axis]
    edge = jnp.zeros_like(lax.slice_in_dim(values, 0, 1, axis=axis))
    return jnp.concatenate([lax.slice_in_dim(values, 1, size, axis=axis), edge], axis)


def plain_dot(operands):
    return jnp.dot(operands[0], operands[1], preferred_element_type=jnp.float32)


def trans_dot(operands):
    return lax.dot_general(operands[0], operands[1], (((1,), (1,)), ((), ())), preferred_element_type=jnp.float32)


def operate(rounded, stiffness, face_rows):
    local_part = lax.map(plain_dot, (rounded, stiffness))
    face_values = jax.vmap(lambda vals, index: jnp.take(vals, index, axis=1))(rounded, face_rows)
    grid = face_values.reshape(N_GX, N_GY, N_GZ, COLUMNS, 6, FACE_DOFS)
    incoming = jnp.stack([
        from_lower(grid[..., 1, :], 0), from_upper(grid[..., 0, :], 0),
        from_lower(grid[..., 3, :], 1), from_upper(grid[..., 2, :], 1),
        from_lower(grid[..., 5, :], 2), from_upper(grid[..., 4, :], 2)], axis=4)
    incoming = incoming.reshape(SUBDOMAINS, COLUMNS, 6 * FACE_DOFS).astype(jnp.float32)
    coupled = jax.vmap(lambda vals, index: jnp.zeros((COLUMNS, INTERFACE), jnp.float32).at[:, index.reshape(-1)].add(vals))(incoming, face_rows)
    return local_part - 0.5 * coupled


def precondition(rounded, stiff_inverse, coarse_basis, coarse_map, group_rows, root_coupling, root_inverse):
    near_part = lax.map(plain_dot, (rounded, stiff_inverse))
    coarse = lax.map(trans_dot, (rounded, coarse_basis)).astype(jnp.bfloat16)
    lifted = jax.vmap(lambda vals, index: jnp.zeros((COLUMNS, GROUP_DOFS), jnp.float32).at[:, index].add(vals.astype(jnp.float32)))(coarse, coarse_map)
    group_total = jnp.sum(lifted.reshape(CHILDREN, GROUPS, COLUMNS, GROUP_DOFS), axis=0)
    root_total = jnp.einsum('src,scn->rn', coarse.astype(jnp.float32), root_coupling.astype(jnp.float32), precision=lax.Precision.HIGHEST)
    group_round = group_total.astype(jnp.bfloat16)
    group_index = (jnp.arange(SUBDOMAINS) % GROUPS).astype(jnp.int32)

    def group_part(operands):
        return lax.dot_general(group_round[operands[1]], operands[0], (((1,), (1,)), ((), ())), preferred_element_type=jnp.float32)

    grouped = lax.map(group_part, (group_rows, group_index))
    solved = jnp.dot(root_total.astype(jnp.bfloat16), root_inverse, preferred_element_type=jnp.float32).astype(jnp.bfloat16)
    from_root = lax.map(lambda coupling: lax.dot_general(solved, coupling, (((1,), (1,)), ((), ())), preferred_element_type=jnp.float32), root_coupling)
    correction = (grouped + from_root).astype(jnp.bfloat16)
    return near_part + lax.map(plain_dot, (correction, coarse_basis))


def reference(loads, stiffness, stiff_inverse, face_rows, coarse_basis, coarse_map, group_rows, root_coupling, root_inverse):
    stiff = stiffness.reshape(SUBDOMAINS, INTERFACE, INTERFACE)
    inverse = stiff_inverse.reshape(SUBDOMAINS, INTERFACE, INTERFACE)
    basis = coarse_basis.reshape(SUBDOMAINS, COARSE, INTERFACE)
    rows_group = group_rows.reshape(SUBDOMAINS, COARSE, GROUP_DOFS)
    coupling = root_coupling.reshape(SUBDOMAINS, COARSE, ROOT_DOFS)
    right_side = split_subs(loads)

    def apply_pre(field):
        return precondition(field.astype(jnp.bfloat16), inverse, basis, coarse_map, rows_group, coupling, root_inverse)

    first = apply_pre(right_side)
    after = right_side - operate(first.astype(jnp.bfloat16), stiff, face_rows)
    solution = first + apply_pre(after)
    residual = right_side - operate(solution.astype(jnp.bfloat16), stiff, face_rows)
    return join_subs(solution), join_subs(residual)
```

```python
import jax
import jax.numpy as jnp
from jax import lax
from jax.sharding import PartitionSpec as P

GROUP_DOFS = 1536
BF16 = jnp.bfloat16
F32 = jnp.float32
RADIX = 64


def dot(a, b, dims):
    return lax.dot_general(a, b, ((dims[0:1], dims[1:2]), ((), ())), preferred_element_type=F32)


def shift_pairs(count):
    up = [(i, i + 1) for i in range(count - 1)]
    return up, [(j, i) for i, j in up]


def exchange_faces(faces):
    received = []
    for d, axis in enumerate(("gx", "gy", "gz")):
        up, down = shift_pairs(lax.axis_size(axis))
        received.append(lax.ppermute(faces[2 * d + 1], axis, up))
        received.append(lax.ppermute(faces[2 * d], axis, down))
    return received


def high_low(values):
    high = lax.reduce_precision(values, 8, 7)
    return jnp.concatenate([high.astype(BF16), (values - high).astype(BF16)], axis=-2)


def rejoin(rows):
    high, low = jnp.split(rows.astype(F32), 2, axis=-2)
    return high + low


def map_rows(coarse_map):
    padded = jnp.pad(coarse_map[0], (0, 64)).reshape(2, 128)
    digits = jnp.concatenate([padded // RADIX, padded % RADIX], axis=0)
    return jnp.pad(digits, ((0, 12), (0, 0))).astype(BF16)


def shards(
    loads,
    stiffness,
    stiff_inverse,
    face_rows,
    coarse_basis,
    coarse_map,
    group_rows,
    root_coupling,
    root_inverse,
):
    columns = loads.shape[0]
    coarse_dofs, root_dofs = root_coupling.shape
    n_gx, n_gy, n_gz = (lax.axis_size(a) for a in ("gx", "gy", "gz"))
    plane = n_gy * n_gz
    part = columns // plane
    chunks = root_dofs // 128
    same_core = [list(range(c, n_gx, 2)) for c in (0, 1)]
    other_core = [(i, i ^ 1) for i in range(n_gx)]
    flat_faces = face_rows[0].reshape(-1)
    select = (flat_faces[:, None] == jnp.arange(loads.shape[1], dtype=jnp.int32)[None, :]).astype(BF16)
    face_count = face_rows.shape[2]
    digits = map_rows(coarse_map)

    def gathered_map(rows):
        values = rows.astype(F32)
        number = values[:, 0:2] * RADIX + values[:, 2:4]
        return number.reshape(rows.shape[0], -1)[:, :coarse_dofs].reshape(-1).astype(jnp.int32)

    def apply_pre(rounded, selector):
        near = dot(rounded, stiff_inverse, (1, 0))
        coarse_t = dot(coarse_basis, rounded, (1, 1)).astype(BF16)
        root_term = dot(coarse_t, root_coupling, (0, 0)).astype(BF16)
        pieces = lax.all_to_all(
            root_term.reshape(plane, part, root_dofs), ("gy", "gz"), 0, 0, tiled=True
        )
        mine = jnp.sum(pieces.astype(F32), axis=0)
        mine = high_low(mine.reshape(part, chunks, 128).transpose(1, 0, 2).reshape(-1, 128))
        own_rows = mine.shape[0]
        parts = [coarse_t, mine] + ([digits] if selector is None else [])
        payload = jnp.concatenate(parts, axis=0)
        everyone = lax.all_gather(payload, "gx", axis_index_groups=same_core)
        top = coarse_dofs + own_rows
        if selector is None:
            numbers = gathered_map(everyone[:, top : top + 4])
            selector = (
                jnp.arange(GROUP_DOFS, dtype=jnp.int32)[:, None] == numbers[None, :]
            ).astype(BF16)
        group_half = dot(selector, everyone[:, :coarse_dofs].reshape(-1, 128), (1, 0))
        root_half = jnp.sum(rejoin(everyone[:, coarse_dofs:top]), axis=0)
        half = jnp.concatenate([group_half.astype(BF16), high_low(root_half)], axis=0)
        other = lax.ppermute(half, "gx", other_core)
        group_total = (half[:GROUP_DOFS].astype(F32) + other[:GROUP_DOFS].astype(F32)).astype(BF16)
        rows = (root_half + rejoin(other[GROUP_DOFS:])).astype(BF16)
        rows = rows.reshape(chunks, part, 128).transpose(1, 0, 2).reshape(part, root_dofs)
        solved = dot(rows, root_inverse, (1, 0)).astype(BF16)
        solved = lax.all_gather(solved, "gz")
        solved = lax.all_gather(solved, "gy").reshape(columns, root_dofs)
        grouped = dot(group_total, group_rows, (0, 1))
        correction = (grouped + dot(solved, root_coupling, (1, 1))).astype(BF16)
        return near + dot(correction, coarse_basis, (1, 0)), selector

    def operate(rounded):
        faces = dot(select, rounded, (1, 1)).astype(BF16)
        faces = [faces[d * face_count : (d + 1) * face_count] for d in range(6)]
        incoming = exchange_faces(faces)
        local = dot(rounded, stiffness, (1, 0))
        coupled = dot(jnp.concatenate(incoming, axis=0), select, (0, 0))
        return local - 0.5 * coupled

    first, selector = apply_pre(loads.astype(BF16), None)
    after = loads - operate(first.astype(BF16))
    change, _ = apply_pre(after.astype(BF16), selector)
    solution = first + change
    residual = loads - operate(solution.astype(BF16))
    return (solution, residual)


def solution(mesh):
    split = ("gx", "gy", "gz")
    rows = P(split, None)
    in_specs = (P(None, split), rows, rows, P(split, None, None), rows, rows, rows, rows, P())
    out_specs = (P(None, split), P(None, split))
    return jax.shard_map(shards, mesh=mesh, in_specs=in_specs, out_specs=out_specs, check_vma=False)
```

```python
import jax
import jax.numpy as jnp
from jax import lax
from jax.sharding import PartitionSpec as P


GROUP_DOFS = 1536
BF16 = jnp.bfloat16
F32 = jnp.float32
RADIX = 64
PLANE = ("gy", "gz")


def dot(a, b, dims):
    return lax.dot_general(a, b, ((dims[0:1], dims[1:2]), ((), ())), preferred_element_type=F32)


def shift_pairs(count):
    up = [(i, i + 1) for i in range(count - 1)]
    return up, [(j, i) for i, j in up]


def exchange_faces(rows):
    width = rows.shape[0] // 6
    faces = [rows[d * width : (d + 1) * width] for d in range(6)]
    received = []
    for d, axis in enumerate(("gx", "gy", "gz")):
        up, down = shift_pairs(lax.axis_size(axis))
        received.append(lax.ppermute(faces[2 * d + 1], axis, up))
        received.append(lax.ppermute(faces[2 * d], axis, down))
    return jnp.concatenate(received, axis=0)


def high_low(values):
    high = lax.reduce_precision(values, 8, 7)
    return jnp.concatenate([high.astype(BF16), (values - high).astype(BF16)], axis=-2)


def rejoin(rows):
    high, low = jnp.split(rows.astype(F32), 2, axis=-2)
    return high + low


def map_rows(coarse_map):
    padded = jnp.pad(coarse_map[0], (0, 64)).reshape(2, 128)
    digits = jnp.concatenate([padded // RADIX, padded % RADIX], axis=0)
    return jnp.pad(digits, ((0, 12), (0, 0))).astype(BF16)


def shards(
    loads,
    stiffness,
    stiff_inverse,
    face_rows,
    coarse_basis,
    coarse_map,
    group_rows,
    root_coupling,
    root_inverse,
):
    coarse_dofs, root_dofs = root_coupling.shape
    n_gx, n_gy, n_gz = (lax.axis_size(a) for a in ("gx", "gy", "gz"))
    plane = n_gy * n_gz
    part = root_dofs // plane
    same_core = [list(range(c, n_gx, 2)) for c in (0, 1)]
    other_core = [(i, i ^ 1) for i in range(n_gx)]
    flat_faces = face_rows[0].reshape(-1)
    select = (flat_faces[:, None] == jnp.arange(loads.shape[1], dtype=jnp.int32)[None, :]).astype(BF16)
    digits = map_rows(coarse_map)
    basis_faces = dot(select, coarse_basis, (1, 1)).astype(BF16)
    root_at_faces = dot(basis_faces, root_coupling, (1, 0)).astype(BF16)

    def gathered_map(rows):
        values = rows.astype(F32)
        number = values[:, 0:2] * RADIX + values[:, 2:4]
        return number.reshape(rows.shape[0], -1)[:, :coarse_dofs].reshape(-1).astype(jnp.int32)

    def apply_pre(rounded, selector):
        near = dot(rounded, stiff_inverse, (1, 0))
        coarse_t = dot(coarse_basis, rounded, (1, 1)).astype(BF16)
        root_term = dot(root_coupling, coarse_t, (0, 0)).astype(BF16)
        pieces = lax.all_to_all(root_term.reshape(plane, part, 128), PLANE, 0, 0, tiled=True)
        parts = [coarse_t] + ([digits] if selector is None else [])
        everyone = lax.all_gather(jnp.concatenate(parts, axis=0), "gx", axis_index_groups=same_core)
        mine = jnp.sum(pieces.astype(F32), axis=0)
        pair = mine + rejoin(lax.ppermute(high_low(mine), "gx", other_core))
        spread = jnp.broadcast_to(high_low(pair)[None], (n_gx // 2, 2 * part, 128))
        lines = lax.all_to_all(spread, "gx", 0, 0, axis_index_groups=same_core, tiled=True)
        root_rows = jnp.sum(rejoin(lines), axis=0)
        spread = jnp.broadcast_to(root_rows.astype(BF16)[None], (plane, part, 128))
        root_total = lax.all_to_all(spread, PLANE, 0, 0, tiled=True).reshape(root_dofs, 128)
        if selector is None:
            numbers = gathered_map(everyone[:, coarse_dofs : coarse_dofs + 4])
            selector = (
                jnp.arange(GROUP_DOFS, dtype=jnp.int32)[:, None] == numbers[None, :]
            ).astype(BF16)
        group_half = dot(selector, everyone[:, :coarse_dofs].reshape(-1, 128), (1, 0)).astype(BF16)
        group_half = lax.optimization_barrier(group_half)
        other = lax.ppermute(group_half, "gx", other_core)
        group_total = (group_half.astype(F32) + other.astype(F32)).astype(BF16)
        grouped = dot(group_rows, group_total, (1, 0)).astype(BF16)
        grouped = lax.optimization_barrier(grouped)
        without_root = near + dot(grouped, coarse_basis, (0, 0))
        solved = dot(root_inverse, root_total, (0, 0)).astype(BF16)
        from_root = dot(root_coupling, solved, (1, 0)).astype(BF16)
        return without_root, dot(from_root, coarse_basis, (0, 0)), solved, selector

    def operate(without_root, total, solved, root_at_neighbours):
        faces = dot(select, without_root.astype(BF16), (1, 1)).astype(BF16)
        if root_at_neighbours is None:
            received = exchange_faces(jnp.concatenate([faces, root_at_faces], axis=1))
            incoming, root_at_neighbours = received[:, :128], received[:, 128:]
        else:
            incoming = exchange_faces(faces)
        coupled = lax.optimization_barrier(dot(incoming, select, (0, 0)))
        at_faces = dot(root_at_neighbours, solved, (1, 0)).astype(BF16)
        local = dot(total.astype(BF16), stiffness, (1, 0))
        return local - 0.5 * (coupled + dot(at_faces, select, (0, 0))), root_at_neighbours

    base, root_part, solved, selector = apply_pre(loads.astype(BF16), None)
    first = base + root_part
    applied, root_at_neighbours = operate(base, first, solved, None)
    after = loads - applied
    change, root_change, solved_change, _ = apply_pre(after.astype(BF16), selector)
    base = base + change
    solved_sum = solved.astype(F32) + solved_change.astype(F32)
    solution = first + (change + root_change)
    applied, _ = operate(base, solution, solved_sum.astype(BF16), root_at_neighbours)
    residual = loads - applied
    return (solution, residual)


def solution(mesh):
    split = ("gx", "gy", "gz")
    rows = P(split, None)
    in_specs = (P(None, split), rows, rows, P(split, None, None), rows, rows, rows, rows, P())
    out_specs = (P(None, split), P(None, split))
    return jax.shard_map(shards, mesh=mesh, in_specs=in_specs, out_specs=out_specs, check_vma=False)
```

```python
import jax
import jax.numpy as jnp
from jax import lax
from jax.sharding import PartitionSpec as P


GROUP_DOFS = 1536
BF16 = jnp.bfloat16
F32 = jnp.float32
RADIX = 64
PLANE = ("gy", "gz")


def dot(a, b, dims):
    return lax.dot_general(a, b, ((dims[0:1], dims[1:2]), ((), ())), preferred_element_type=F32)


def shift_pairs(count):
    up = [(i, i + 1) for i in range(count - 1)]
    return up, [(j, i) for i, j in up]


def exchange_faces(rows):
    width = rows.shape[0] // 6
    faces = [rows[d * width : (d + 1) * width] for d in range(6)]
    received = []
    for d, axis in enumerate(("gx", "gy", "gz")):
        up, down = shift_pairs(lax.axis_size(axis))
        received.append(lax.ppermute(faces[2 * d + 1], axis, up))
        received.append(lax.ppermute(faces[2 * d], axis, down))
    return jnp.concatenate(received, axis=0)


def high_low(values):
    high = lax.reduce_precision(values, 8, 7)
    return jnp.concatenate([high.astype(BF16), (values - high).astype(BF16)], axis=-2)


def rejoin(rows):
    high, low = jnp.split(rows.astype(F32), 2, axis=-2)
    return high + low


def map_rows(coarse_map):
    padded = jnp.pad(coarse_map[0], (0, 64)).reshape(2, 128)
    digits = jnp.concatenate([padded // RADIX, padded % RADIX], axis=0)
    return jnp.pad(digits, ((0, 12), (0, 0))).astype(BF16)


def shards(
    loads,
    stiffness,
    stiff_inverse,
    face_rows,
    coarse_basis,
    coarse_map,
    group_rows,
    root_coupling,
    root_inverse,
):
    coarse_dofs, root_dofs = root_coupling.shape
    n_gx, n_gy, n_gz = (lax.axis_size(a) for a in ("gx", "gy", "gz"))
    plane = n_gy * n_gz
    part = root_dofs // plane
    same_core = [list(range(c, n_gx, 2)) for c in (0, 1)]
    other_core = [(i, i ^ 1) for i in range(n_gx)]
    flat_faces = face_rows[0].reshape(-1)
    select = (flat_faces[:, None] == jnp.arange(loads.shape[1], dtype=jnp.int32)[None, :]).astype(BF16)
    select = lax.optimization_barrier(select)
    digits = map_rows(coarse_map)
    basis_faces = dot(select, coarse_basis, (1, 1)).astype(BF16)
    root_at_faces = dot(basis_faces, root_coupling, (1, 0)).astype(BF16)

    def gathered_map(rows):
        values = rows.astype(F32)
        number = values[:, 0:2] * RADIX + values[:, 2:4]
        return number.reshape(rows.shape[0], -1)[:, :coarse_dofs].reshape(-1).astype(jnp.int32)

    def swap(blocks, axes):
        return lax.all_to_all(blocks, axes, 0, 0, tiled=True)

    def reduce_plane(rows, staged):
        if not staged:
            pieces = swap(rows.reshape(plane, part, 128), PLANE)
            return jnp.sum(pieces.astype(F32), axis=0)
        pieces = swap(rows.reshape(n_gz, n_gy * part, 128), "gz")
        kept = high_low(jnp.sum(pieces.astype(F32), axis=0).reshape(n_gy, part, 128))
        pieces = swap(kept, "gy")
        return jnp.sum(rejoin(pieces), axis=0)

    def spread_plane(rows, staged):
        if not staged:
            return swap(jnp.broadcast_to(rows[None], (plane,) + rows.shape), PLANE).reshape(root_dofs, 128)
        rows = swap(jnp.broadcast_to(rows[None], (n_gy,) + rows.shape), "gy").reshape(-1, 128)
        return swap(jnp.broadcast_to(rows[None], (n_gz,) + rows.shape), "gz").reshape(root_dofs, 128)

    def apply_pre(rounded, selector):
        staged = selector is not None
        near = dot(rounded, stiff_inverse, (1, 0))
        coarse_t = dot(coarse_basis, rounded, (1, 1)).astype(BF16)
        root_term = dot(root_coupling, coarse_t, (0, 0)).astype(BF16)
        mine = high_low(reduce_plane(root_term, staged))
        top = coarse_dofs + mine.shape[0]
        parts = [coarse_t, mine] + ([digits] if selector is None else [])
        payload = jnp.concatenate(parts, axis=0)
        if staged:
            payload = lax.optimization_barrier(payload.reshape(-1, 16, 128))
            everyone = lax.optimization_barrier(lax.all_gather(payload[None], "gx", axis_index_groups=same_core, axis=0, tiled=True))
            everyone = everyone.reshape(n_gx // 2, -1, 128)
        else:
            everyone = lax.all_gather(payload, "gx", axis_index_groups=same_core)
        root_half = jnp.sum(rejoin(everyone[:, coarse_dofs:top]), axis=0)
        root_rows = root_half + rejoin(lax.ppermute(high_low(root_half), "gx", other_core))
        root_total = spread_plane(root_rows.astype(BF16), staged)
        if selector is None:
            numbers = gathered_map(everyone[:, top : top + 4])
            selector = (
                jnp.arange(GROUP_DOFS, dtype=jnp.int32)[:, None] == numbers[None, :]
            ).astype(BF16)
        group_half = dot(selector, everyone[:, :coarse_dofs].reshape(-1, 128), (1, 0)).astype(BF16)
        group_half = lax.optimization_barrier(group_half)
        other = lax.ppermute(group_half, "gx", other_core)
        group_total = (group_half.astype(F32) + other.astype(F32)).astype(BF16)
        grouped = dot(group_rows, group_total, (1, 0)).astype(BF16)
        grouped = lax.optimization_barrier(grouped)
        without_root = near + dot(grouped, coarse_basis, (0, 0))
        solved = dot(root_inverse, root_total, (0, 0)).astype(BF16)
        from_root = dot(root_coupling, solved, (1, 0)).astype(BF16)
        return without_root, dot(from_root, coarse_basis, (0, 0)), solved, selector

    def operate(without_root, total, solved, root_at_neighbours):
        faces = dot(select, without_root.astype(BF16), (1, 1)).astype(BF16)
        if root_at_neighbours is None:
            received = exchange_faces(jnp.concatenate([faces, root_at_faces], axis=1))
            incoming, root_at_neighbours = received[:, :128], received[:, 128:]
        else:
            incoming = exchange_faces(faces)
        coupled = lax.optimization_barrier(dot(incoming, select, (0, 0)))
        at_faces = dot(root_at_neighbours, solved, (1, 0)).astype(BF16)
        local = dot(total.astype(BF16), stiffness, (1, 0))
        return local - 0.5 * (coupled + dot(at_faces, select, (0, 0))), root_at_neighbours

    base, root_part, solved, selector = apply_pre(loads.astype(BF16), None)
    first = base + root_part
    applied, root_at_neighbours = operate(base, first, solved, None)
    after = loads - applied
    change, root_change, solved_change, _ = apply_pre(after.astype(BF16), selector)
    base = base + change
    solved_sum = solved.astype(F32) + solved_change.astype(F32)
    solution = first + (change + root_change)
    applied, _ = operate(base, solution, solved_sum.astype(BF16), root_at_neighbours)
    residual = loads - applied
    return (solution, residual)


def solution(mesh):
    split = ("gx", "gy", "gz")
    rows = P(split, None)
    in_specs = (P(None, split), rows, rows, P(split, None, None), rows, rows, rows, rows, P())
    out_specs = (P(None, split), P(None, split))
    return jax.shard_map(shards, mesh=mesh, in_specs=in_specs, out_specs=out_specs, check_vma=False)
```
